32 devices in a mesh: groups: 2 (over y), tm: 4 (over z), rows: 4 (over x, core).
Axes of the slice: x: 2, y: 2, z: 4, core: 2. Of those that a mesh axis runs over, the one named last changes fastest.
Arguments:
- inputs: bfloat16 [8, 16, 4, 19968], P('groups', 'tm', 'rows'), parts along dimension 0, may hold values from -6 to 6
- cotangent: bfloat16 [8, 16, 4, 19968], P('groups', 'tm', 'rows'), parts along dimension 0, may hold values from -6 to 6
- kernel: bfloat16 [27, 192, 192], replicated, may hold values from -0.078125 to 0.078125
- span_frames: int32 [8], P('groups'), parts along dimension 0, may hold values from 1 to 4, as said below
Outputs:
- grad_inputs: bfloat16 [8, 16, 4, 19968], P('groups', 'tm', 'rows'), parts along dimension 0
- weight_grad: float32 [54, 192, 192], P('groups', 'tm', 'rows'), parts along dimension 0
The draws below stay inside these ranges and needn't reach their ends.
There are 2 independent parts, one for each index of `groups`. The reference program is written for one: setup_inputs(seed, part) draws one part's arguments, and reference() takes and returns one part's arrays. A program takes and returns all parts, laid end to end along the dimension named above; an argument that names none is the same for every part. Nothing has to cross between parts.
Inputs may be any that keep to these rules, and one draw needn't show every extreme that they name: Entry 0 is 1. Time span c holds span_frames[c] consecutive frames of every video in its first slots, the frames following those of span c - 1; its other slots hold no frame, and inputs and cotangent there are not read.
All inputs are finite; a program needn't handle non-finite values.
Results may differ from the reference program's by a relative error of at most 0.0031.
Values may be sent and summed in bfloat16 or wider, within the bound.
A program may use at most 192 MiB of HBM per device.

```python
import jax
import jax.numpy as jnp
from jax import lax

CH = 192
TAPS = 27
GRID_W = 104
BATCH = 4
SLOTS_DEV = 4
SPANS = 4
SLOTS = 16
HEIGHT = 4
CELLS = 26624


def draw_span_frames(key, part):
    key_counts = jax.random.fold_in(key, 101)
    key_order = jax.random.fold_in(key, 202)
    counts = jax.random.randint(key_counts, (SPANS,), 1, SLOTS_DEV + 1).astype(jnp.int32)
    shuffled = jax.random.permutation(key_order, SPANS - 1).astype(jnp.int32) + 1
    chosen = shuffled[0]
    order = jnp.arange(SPANS, dtype=jnp.int32)
    counts = jnp.where(order == chosen, SLOTS_DEV, counts)
    counts = jnp.where(order == 0, 1, counts)
    return counts.astype(jnp.int32)


def level_of(own_key, shape, cuts, least, high):
    def one(position, blocks):
        heights = jax.random.uniform(jax.random.fold_in(jax.random.fold_in(own_key, 6), position), (blocks,), jnp.float32, least / len(cuts), high / len(cuts))
        return jnp.repeat(jnp.exp(heights), shape[position] // blocks).reshape((-1,) + (1,) * (len(shape) - position - 1))

    factor_of = one(*cuts[0])
    for cut in cuts[1:]:
        factor_of = factor_of * one(*cut)
    return factor_of


def bell_draw(rng, dims, width, most, shards=(), kind=jnp.bfloat16):
    entries = width * jax.random.normal(rng, dims, jnp.float32)
    if shards:
        entries = entries * level_of(rng, dims, shards, -0.22, 0.18)
    return jnp.clip(entries, -most, most).astype(kind)


def setup_inputs(seed: int = 0, part: int = 0) -> dict:
    key_list = jax.random.split(jax.random.key(seed), 5)
    part_keys = jax.random.split(jax.random.fold_in(key_list[4], part), 5)
    inputs = bell_draw(part_keys[0], (BATCH, SLOTS, HEIGHT, GRID_W * CH), 1.0, 6.0, ((1, 4), (2, 4)))
    cotangent = bell_draw(part_keys[1], (BATCH, SLOTS, HEIGHT, GRID_W * CH), 1.0, 6.0, ((1, 4), (2, 4)))
    kernel = bell_draw(key_list[2], (TAPS, CH, CH), (TAPS * CH) ** -0.5, 0.078125)
    span_frames = draw_span_frames(jax.random.fold_in(jax.random.fold_in(key_list[4], part), 71), part)
    return {"inputs": inputs, "cotangent": cotangent, "kernel": kernel, "span_frames": span_frames}


def reference(inputs, cotangent, kernel, span_frames):
    batch, slots, height, flat = inputs.shape
    per_span = slots // SPANS
    starts = (jnp.cumsum(span_frames) - span_frames).astype(jnp.int32)
    slot_ids = jnp.arange(slots, dtype=jnp.int32)
    span_ids = (slot_ids // per_span).astype(jnp.int32)
    within = (slot_ids % per_span).astype(jnp.int32)
    live = within < span_frames[span_ids]
    target = jnp.where(live, starts[span_ids] + within, slots).astype(jnp.int32)
    values = inputs.astype(jnp.float32)
    sigma = jax.nn.sigmoid(values)
    silu_out = (values * sigma).astype(jnp.bfloat16)
    compact_act = jnp.zeros_like(silu_out).at[:, target].set(silu_out, mode="drop")
    compact_grad = jnp.zeros_like(cotangent).at[:, target].set(cotangent, mode="drop")
    act_pad = jnp.pad(compact_act.reshape(batch, slots, height, GRID_W, CH), ((0, 0), (2, 0), (1, 1), (1, 1), (0, 0)))
    grad_pad = jnp.pad(compact_grad.reshape(batch, slots, height, GRID_W, CH), ((0, 0), (0, 2), (1, 1), (1, 1), (0, 0)))
    grad_flat = compact_grad.reshape(-1, CH)
    cell_count = grad_flat.shape[0]
    adjoint = jnp.zeros((cell_count, CH), jnp.float32)
    pieces = []
    for frame_off in range(3):
        for row_off in range(3):
            for col_off in range(3):
                tap_index = 9 * frame_off + 3 * row_off + col_off
                window = act_pad[:, frame_off:frame_off + slots, row_off:row_off + height, col_off:col_off + GRID_W].reshape(cell_count, CH)
                pieces.append(lax.dot_general(window, grad_flat, (((0,), (0,)), ((), ())), preferred_element_type=jnp.float32))
                mirror = grad_pad[:, 2 - frame_off:2 - frame_off + slots, 2 - row_off:2 - row_off + height, 2 - col_off:2 - col_off + GRID_W].reshape(cell_count, CH)
                adjoint = adjoint + lax.dot_general(mirror, kernel[tap_index], (((1,), (1,)), ((), ())), preferred_element_type=jnp.float32)
    adjoint = adjoint.reshape(batch, slots, height, flat)
    gathered = adjoint[:, jnp.minimum(target, slots - 1)]
    slope = sigma * (1.0 + values * (1.0 - sigma))
    mask = live[None, :, None, None]
    grad_inputs = jnp.where(mask, gathered * slope, jnp.zeros_like(slope)).astype(jnp.bfloat16)
    weight_grad = jnp.stack(pieces) * (CELLS ** -0.5)
    return grad_inputs, weight_grad
```

```python
import functools

import jax
import jax.numpy as jnp
from jax import lax
from jax.experimental import pallas as pl
from jax.experimental.pallas import tpu as pltpu
from jax.sharding import PartitionSpec as P

CH = 192
PAIR = 2 * CH
MESH = pl.DeviceIdType.MESH


def local_kernel(cells, strips, x_ref, mask_ref, grad_ref, kern_ref, out_ref, wg_ref, xc, act, act3, gc):
    frames = x_ref.shape[0]
    pairs = cells // 2
    wide = CH // strips
    live = mask_ref[...] > 0.5

    def split(p, carry):
        at = pl.multiple_of(p * PAIR, 128)
        v = x_ref[:, pl.ds(at, PAIR)]
        for q in range(2):
            cell = v[:, q * CH:(q + 1) * CH]
            xc[2 * p + q] = cell
            xf = cell.astype(jnp.float32)
            s = 1.0 / (1.0 + jnp.exp(-xf))
            act[2 * p + q + 1] = jnp.where(live, xf * s, 0.0).astype(jnp.bfloat16)
        for k in range(9):
            g = grad_ref[k, :, pl.ds(at, PAIR)]
            gc[k, 2 * p + 1] = g[:, :CH]
            gc[k, 2 * p + 2] = g[:, CH:]
        return carry

    zero = jnp.zeros((frames, CH), jnp.bfloat16)
    for end in (0, cells + 1):
        act[end] = zero
        for k in range(9):
            gc[k, end] = zero
    lax.fori_loop(0, pairs, split, 0)

    def widen(w, carry):
        act3[w] = jnp.concatenate([act[w], act[w + 1], act[w + 2]], axis=1)
        return carry

    lax.fori_loop(0, cells, widen, 0)
    a3 = act3[...].reshape(cells * frames, 3 * CH)

    def weight(k, carry):
        g = gc[k, pl.ds(1, cells)].reshape(cells * frames, CH)
        res = lax.dot_general(g, a3, (((0,), (0,)), ((), ())), preferred_element_type=jnp.float32)
        for r in range(strips):
            wg_ref[r, k] = res[r * wide:(r + 1) * wide]
        return carry

    lax.fori_loop(0, 9, weight, 0)

    step = 26 if cells % 26 == 0 else 2

    def adjoint(j, carry):
        w0 = j * step
        acc = jnp.zeros((step * frames, CH), jnp.float32)
        for k in range(9):
            for c in range(3):
                g = gc[k, pl.ds(w0 + 2 - c, step)].reshape(step * frames, CH)
                acc = acc + lax.dot_general(
                    g, kern_ref[3 * k + c], (((1,), (1,)), ((), ())), preferred_element_type=jnp.float32
                )
        acc = acc.reshape(step, frames, CH)
        xf = xc[pl.ds(w0, step)].astype(jnp.float32)
        s = 1.0 / (1.0 + jnp.exp(-xf))
        res = jnp.where(live[None], acc * (s * (1.0 + xf * (1.0 - s))), 0.0).astype(jnp.bfloat16)
        for p in range(step // 2):
            at = pl.multiple_of((w0 + 2 * p) * CH, 128)
            out_ref[:, pl.ds(at, PAIR)] = jnp.concatenate([res[2 * p], res[2 * p + 1]], axis=1)
        return carry

    lax.fori_loop(0, cells // step, adjoint, 0)


def reduce_kernel(strips, spans, factor, wg_ref, out_ref, got1, send2, got2, zfull, zsend, got3, s1, r1, s2, r2, s3, r3):
    row = lax.axis_index("rows")
    span = lax.axis_index("tm")
    half = strips // 2
    place = row // 2
    parity = row - 2 * place
    other = 1 - parity
    partner = 2 * place + other
    part = CH // spans
    taps, wide = wg_ref.shape[1], wg_ref.shape[2]

    def strip_at(d):
        return lax.rem(place + d, half)

    barrier = pltpu.get_barrier_semaphore()
    pl.semaphore_signal(barrier, inc=1, device_id={"rows": partner}, device_id_type=MESH)
    for d in range(1, half):
        pl.semaphore_signal(barrier, inc=1, device_id={"rows": 2 * strip_at(d) + parity}, device_id_type=MESH)
    for d in range(1, spans):
        pl.semaphore_signal(barrier, inc=1, device_id={"tm": lax.rem(span + d, spans)}, device_id_type=MESH)
    pl.semaphore_wait(barrier, half + spans - 1)

    order = list(range(1, half)) + [0]
    first = []
    for d in order:
        k = strip_at(d)
        cp = pltpu.make_async_remote_copy(
            wg_ref.at[2 * k + other], got1.at[d], s1.at[d], r1.at[d],
            device_id={"rows": partner}, device_id_type=MESH,
        )
        cp.start()
        first.append(cp)
    second = []
    for d, cp in zip(order, first):
        cp.wait()
        if d:
            k = strip_at(d)
            send2[d - 1] = (wg_ref[2 * k + parity] + got1[d]).astype(jnp.bfloat16)
            nxt = pltpu.make_async_remote_copy(
                send2.at[d - 1], got2.at[d - 1], s2.at[d - 1], r2.at[d - 1],
                device_id={"rows": 2 * k + parity}, device_id_type=MESH,
            )
            nxt.start()
            second.append(nxt)
    total = wg_ref[row] + got1[0]
    for d, cp in enumerate(second):
        cp.wait()
        total = total + got2[d].astype(jnp.float32)
    turned = total.reshape(taps * wide, 3 * CH).T
    for t in range(spans):
        for c in range(3):
            piece = turned[c * CH + t * part:c * CH + (t + 1) * part]
            zfull[t, c] = piece
            zsend[t, c] = piece.astype(jnp.bfloat16)
    third = []
    for d in range(1, spans):
        to = lax.rem(span + d, spans)
        cp = pltpu.make_async_remote_copy(
            zsend.at[to], got3.at[d - 1], s3.at[d - 1], r3.at[d - 1],
            device_id={"tm": to}, device_id_type=MESH,
        )
        cp.start()
        third.append(cp)
    final = zfull[span]
    for d, cp in enumerate(third):
        cp.wait()
        final = final + got3[d].astype(jnp.float32)
    out_ref[...] = final * factor


def body(inputs, cotangent, kernel, span_frames):
    batch, slots, strip, flat = inputs.shape
    cells = flat // CH
    frames = batch * slots
    assert strip == 1 and cells % 2 == 0 and frames % 16 == 0
    spans, strips = lax.axis_size("tm"), lax.axis_size("rows")
    assert strips % 2 == 0 and CH % spans == 0 and CH % strips == 0
    span = lax.axis_index("tm")
    count = jnp.sum(jnp.where(jnp.arange(span_frames.shape[0], dtype=jnp.int32) == span, span_frames, 0))
    x = inputs.reshape(batch, slots, flat)
    cot = cotangent.reshape(batch, slots, flat)

    back = [(i + 1, i) for i in range(spans - 1)]
    after_one = lax.ppermute(cot[:, 0], "tm", back)
    after_two = lax.ppermute(jnp.where(count >= 2, cot[:, 1], after_one), "tm", back)
    order = jnp.arange(slots + 2, dtype=jnp.int32)[None, :, None]
    ext = jnp.pad(cot, ((0, 0), (0, 2), (0, 0)))
    ext = jnp.where(order < count, ext, jnp.zeros_like(ext))
    ext = jnp.where(order == count, after_one[:, None], ext)
    ext = jnp.where(order == count + 1, after_two[:, None], ext)
    up = [(i, i + 1) for i in range(strips - 1)]
    down = [(i + 1, i) for i in range(strips - 1)]
    above = lax.ppermute(ext, "rows", up)
    below = lax.ppermute(ext, "rows", down)
    rows = (below, ext, above)
    grads = jnp.stack([
        rows[b][:, 2 - a:2 - a + slots].reshape(frames, flat) for a in range(3) for b in range(3)
    ])
    live = jnp.broadcast_to((jnp.arange(slots, dtype=jnp.int32) < count)[None, :, None], (batch, slots, CH))
    mask = live.astype(jnp.float32).reshape(frames, CH)

    vmem = pl.BlockSpec(memory_space=pltpu.VMEM)
    wide, part = CH // strips, CH // spans
    grad_in, wg = pl.pallas_call(
        functools.partial(local_kernel, cells, strips),
        out_shape=(
            jax.ShapeDtypeStruct((frames, flat), jnp.bfloat16),
            jax.ShapeDtypeStruct((strips, 9, wide, 3 * CH), jnp.float32),
        ),
        in_specs=[vmem] * 4,
        out_specs=(vmem, vmem),
        scratch_shapes=[
            pltpu.VMEM((cells, frames, CH), jnp.bfloat16),
            pltpu.VMEM((cells + 2, frames, CH), jnp.bfloat16),
            pltpu.VMEM((cells, frames, 3 * CH), jnp.bfloat16),
            pltpu.VMEM((9, cells + 2, frames, CH), jnp.bfloat16),
        ],
        compiler_params=pltpu.CompilerParams(vmem_limit_bytes=52 << 20),
        name="local",
    )(x.reshape(frames, flat), mask, grads, kernel)

    half = strips // 2
    total_cells = batch * slots * spans * strip * strips * cells
    block = (9, wide, 3 * CH)
    zblock = (3, part, 9 * wide)
    dma = pltpu.SemaphoreType.DMA
    few, some = max(half - 1, 1), max(spans - 1, 1)
    share = pl.pallas_call(
        functools.partial(reduce_kernel, strips, spans, float(total_cells) ** -0.5),
        out_shape=jax.ShapeDtypeStruct(zblock, jnp.float32),
        in_specs=[vmem],
        out_specs=vmem,
        scratch_shapes=[
            pltpu.VMEM((half,) + block, jnp.float32),
            pltpu.VMEM((few,) + block, jnp.bfloat16),
            pltpu.VMEM((few,) + block, jnp.bfloat16),
            pltpu.VMEM((spans,) + zblock, jnp.float32),
            pltpu.VMEM((spans,) + zblock, jnp.bfloat16),
            pltpu.VMEM((some,) + zblock, jnp.bfloat16),
            dma((half,)), dma((half,)), dma((few,)), dma((few,)), dma((some,)), dma((some,)),
        ],
        compiler_params=pltpu.CompilerParams(
            vmem_limit_bytes=52 << 20, collective_id=0, has_side_effects=True
        ),
        name="reduce",
    )(wg)
    share = share.reshape(3, part, 9, wide).transpose(2, 0, 1, 3).reshape(27, part, wide)
    return grad_in.reshape(batch, slots, strip, flat), share


def solution(mesh):
    return jax.shard_map(
        body,
        mesh=mesh,
        in_specs=(
            P("groups", "tm", "rows", None),
            P("groups", "tm", "rows", None),
            P(),
            P("groups"),
        ),
        out_specs=(P("groups", "tm", "rows", None), P("groups", "tm", "rows")),
        check_vma=False,
    )
```

```python
import functools

import jax
import jax.numpy as jnp
from jax import lax
from jax.experimental import pallas as pl
from jax.experimental.pallas import tpu as pltpu
from jax.sharding import PartitionSpec as P

CH = 192
PAIR = 2 * CH
MESH = pl.DeviceIdType.MESH

CUTS = ((0, 5), (5, 9))


def kernel_body(cells, strips, spans, factor, x_ref, mask_ref, below_ref, own_ref, above_ref, kern_ref,
                out_ref, share0_ref, share1_ref, xc, act, act3, gc, wg, got1, send2, got2,
                zfull0, zfull1, zsend0, zsend1, got30, got31, s1, r1, s2, r2, s3, r3):
    frames = x_ref.shape[0]
    tail = own_ref.shape[0] - frames
    batch = tail // 2
    pairs = cells // 2
    wide, part, half = CH // strips, CH // spans, strips // 2
    share, zfull, zsend, got3 = (share0_ref, share1_ref), (zfull0, zfull1), (zsend0, zsend1), (got30, got31)
    row = lax.axis_index("rows")
    span = lax.axis_index("tm")
    place = row // 2
    parity = row - 2 * place
    other = 1 - parity
    partner = 2 * place + other

    def strip_at(d):
        return lax.rem(place + d, half)

    barrier = pltpu.get_barrier_semaphore()
    pl.semaphore_signal(barrier, inc=1, device_id={"rows": partner}, device_id_type=MESH)
    for d in range(1, half):
        pl.semaphore_signal(barrier, inc=1, device_id={"rows": 2 * strip_at(d) + parity}, device_id_type=MESH)
    for d in range(1, spans):
        pl.semaphore_signal(barrier, inc=1, device_id={"tm": lax.rem(span + d, spans)}, device_id_type=MESH)

    live = mask_ref[...] > 0.5
    grads = (below_ref, own_ref, above_ref)

    def split(p, carry):
        at = pl.multiple_of(p * PAIR, 128)
        v = x_ref[:, pl.ds(at, PAIR)]
        for q in range(2):
            cell = v[:, q * CH:(q + 1) * CH]
            xc[2 * p + q] = cell
            xf = cell.astype(jnp.float32)
            s = 1.0 / (1.0 + jnp.exp(-xf))
            act[2 * p + q + 1] = jnp.where(live, xf * s, 0.0).astype(jnp.bfloat16)
        for b in range(3):
            v = grads[b][:, pl.ds(at, PAIR)]
            for q in range(2):
                cell = v[:, q * CH:(q + 1) * CH]
                for a in range(3):
                    lo = (2 - a) * batch
                    gc[3 * a + b, 2 * p + q + 1] = cell[lo:lo + frames]
        return carry

    zero = jnp.zeros((frames, CH), jnp.bfloat16)
    for end in (0, cells + 1):
        act[end] = zero
        for k in range(9):
            gc[k, end] = zero
    lax.fori_loop(0, pairs, split, 0)

    def widen(w, carry):
        act3[w] = jnp.concatenate([act[w], act[w + 1], act[w + 2]], axis=1)
        return carry

    lax.fori_loop(0, cells, widen, 0)
    order = list(range(1, half)) + [0]
    copies1, copies2, copies3 = {}, {}, {}

    def weight(k, carry):
        g = gc[k, pl.ds(1, cells)].reshape(cells * frames, CH)
        a3 = act3[...].reshape(cells * frames, 3 * CH)
        res = lax.dot_general(g, a3, (((0,), (0,)), ((), ())), preferred_element_type=jnp.float32)
        for r in range(strips):
            wg[r, k] = res[r * wide:(r + 1) * wide]
        return carry

    def start_core(n):
        k0, k1 = CUTS[n]
        copies1[n] = []
        for d in order:
            cp = pltpu.make_async_remote_copy(
                wg.at[2 * strip_at(d) + other, pl.ds(k0, k1 - k0)], got1.at[d, pl.ds(k0, k1 - k0)],
                s1.at[n, d], r1.at[n, d], device_id={"rows": partner}, device_id_type=MESH,
            )
            cp.start()
            copies1[n].append(cp)

    def start_rows(n):
        k0, k1 = CUTS[n]
        copies2[n] = []
        for d, cp in zip(order, copies1[n]):
            cp.wait()
            if d:
                to = 2 * strip_at(d) + parity
                send2[d - 1, k0:k1] = (wg[to, k0:k1] + got1[d, k0:k1]).astype(jnp.bfloat16)
                nxt = pltpu.make_async_remote_copy(
                    send2.at[d - 1, pl.ds(k0, k1 - k0)], got2.at[d - 1, pl.ds(k0, k1 - k0)],
                    s2.at[n, d - 1], r2.at[n, d - 1], device_id={"rows": to}, device_id_type=MESH,
                )
                nxt.start()
                copies2[n].append(nxt)

    def start_spans(n):
        k0, k1 = CUTS[n]
        total = wg[row, k0:k1] + got1[0, k0:k1]
        for d, cp in enumerate(copies2[n]):
            cp.wait()
            total = total + got2[d, k0:k1].astype(jnp.float32)
        turned = total.reshape((k1 - k0) * wide, 3 * CH).T
        for t in range(spans):
            for c in range(3):
                piece = turned[c * CH + t * part:c * CH + (t + 1) * part]
                zfull[n][t, c] = piece
                zsend[n][t, c] = piece.astype(jnp.bfloat16)
        copies3[n] = []
        for d in range(1, spans):
            to = lax.rem(span + d, spans)
            cp = pltpu.make_async_remote_copy(
                zsend[n].at[to], got3[n].at[d - 1], s3.at[n, d - 1], r3.at[n, d - 1],
                device_id={"tm": to}, device_id_type=MESH,
            )
            cp.start()
            copies3[n].append(cp)

    def finish(n):
        final = zfull[n][span]
        for d, cp in enumerate(copies3[n]):
            cp.wait()
            final = final + got3[n][d].astype(jnp.float32)
        share[n][...] = final * factor

    step = 26 if cells % 26 == 0 else 2
    steps = cells // step

    def adjoint(j, carry):
        w0 = j * step
        acc = jnp.zeros((step * frames, CH), jnp.float32)
        for k in range(9):
            for c in range(3):
                g = gc[k, pl.ds(w0 + 2 - c, step)].reshape(step * frames, CH)
                acc = acc + lax.dot_general(
                    g, kern_ref[3 * k + c], (((1,), (1,)), ((), ())), preferred_element_type=jnp.float32
                )
        acc = acc.reshape(step, frames, CH)
        xf = xc[pl.ds(w0, step)].astype(jnp.float32)
        s = 1.0 / (1.0 + jnp.exp(-xf))
        res = jnp.where(live[None], acc * (s * (1.0 + xf * (1.0 - s))), 0.0).astype(jnp.bfloat16)
        for p in range(step // 2):
            at = pl.multiple_of((w0 + 2 * p) * CH, 128)
            out_ref[:, pl.ds(at, PAIR)] = jnp.concatenate([res[2 * p], res[2 * p + 1]], axis=1)
        return carry

    lax.fori_loop(*CUTS[0], weight, 0)
    pl.semaphore_wait(barrier, half + spans - 1)
    start_core(0)
    lax.fori_loop(*CUTS[1], weight, 0)
    start_core(1)
    start_rows(0)
    lax.fori_loop(0, steps // 4, adjoint, 0)
    start_rows(1)
    lax.fori_loop(steps // 4, 3 * steps // 4, adjoint, 0)
    start_spans(0)
    lax.fori_loop(3 * steps // 4, steps, adjoint, 0)
    start_spans(1)
    finish(0)
    finish(1)


def body(inputs, cotangent, kernel, span_frames):
    batch, slots, strip, flat = inputs.shape
    cells = flat // CH
    frames = batch * slots
    assert strip == 1 and cells % 2 == 0 and frames % 16 == 0
    spans, strips = lax.axis_size("tm"), lax.axis_size("rows")
    assert strips % 2 == 0 and CH % spans == 0 and CH % strips == 0
    span = lax.axis_index("tm")
    count = jnp.sum(jnp.where(jnp.arange(span_frames.shape[0], dtype=jnp.int32) == span, span_frames, 0))
    x = inputs.reshape(batch, slots, flat).transpose(1, 0, 2).reshape(frames, flat)
    cot = cotangent.reshape(batch, slots, flat).transpose(1, 0, 2)

    back = [(i + 1, i) for i in range(spans - 1)]
    after_one = lax.ppermute(cot[0], "tm", back)
    after_two = lax.ppermute(jnp.where(count >= 2, cot[1], after_one), "tm", back)
    order = jnp.arange(slots + 2, dtype=jnp.int32)[:, None, None]
    ext = jnp.pad(cot, ((0, 2), (0, 0), (0, 0)))
    ext = jnp.where(order < count, ext, jnp.zeros_like(ext))
    ext = jnp.where(order == count, after_one[None], ext)
    ext = jnp.where(order == count + 1, after_two[None], ext)
    ext = ext.reshape(frames + 2 * batch, flat)
    up = [(i, i + 1) for i in range(strips - 1)]
    down = [(i + 1, i) for i in range(strips - 1)]
    above = lax.ppermute(ext, "rows", up)
    below = lax.ppermute(ext, "rows", down)
    live = jnp.arange(frames, dtype=jnp.int32) < count * batch
    mask = jnp.broadcast_to(live[:, None], (frames, CH)).astype(jnp.float32)

    vmem = pl.BlockSpec(memory_space=pltpu.VMEM)
    wide, part, half = CH // strips, CH // spans, strips // 2
    total_cells = batch * slots * spans * strip * strips * cells
    few, some = max(half - 1, 1), max(spans - 1, 1)
    sizes = [k1 - k0 for k0, k1 in CUTS]
    zblocks = [(3, part, n * wide) for n in sizes]
    dma = pltpu.SemaphoreType.DMA
    block = (9, wide, 3 * CH)
    grad_in, *shares = pl.pallas_call(
        functools.partial(kernel_body, cells, strips, spans, float(total_cells) ** -0.5),
        out_shape=(
            jax.ShapeDtypeStruct((frames, flat), jnp.bfloat16),
            jax.ShapeDtypeStruct(zblocks[0], jnp.float32),
            jax.ShapeDtypeStruct(zblocks[1], jnp.float32),
        ),
        in_specs=[vmem] * 6,
        out_specs=(vmem, vmem, vmem),
        scratch_shapes=[
            pltpu.VMEM((cells, frames, CH), jnp.bfloat16),
            pltpu.VMEM((cells + 2, frames, CH), jnp.bfloat16),
            pltpu.VMEM((cells, frames, 3 * CH), jnp.bfloat16),
            pltpu.VMEM((9, cells + 2, frames, CH), jnp.bfloat16),
            pltpu.VMEM((strips,) + block, jnp.float32),
            pltpu.VMEM((half,) + block, jnp.float32),
            pltpu.VMEM((few,) + block, jnp.bfloat16),
            pltpu.VMEM((few,) + block, jnp.bfloat16),
            pltpu.VMEM((spans,) + zblocks[0], jnp.float32),
            pltpu.VMEM((spans,) + zblocks[1], jnp.float32),
            pltpu.VMEM((spans,) + zblocks[0], jnp.bfloat16),
            pltpu.VMEM((spans,) + zblocks[1], jnp.bfloat16),
            pltpu.VMEM((some,) + zblocks[0], jnp.bfloat16),
            pltpu.VMEM((some,) + zblocks[1], jnp.bfloat16),
            dma((2, half)), dma((2, half)), dma((2, few)), dma((2, few)), dma((2, some)), dma((2, some)),
        ],
        compiler_params=pltpu.CompilerParams(
            vmem_limit_bytes=56 << 20, collective_id=0, has_side_effects=True
        ),
        name="fused",
    )(x, mask, below, ext, above, kernel)
    share = jnp.concatenate([s.reshape(3, part, n, wide) for s, n in zip(shares, sizes)], axis=2)
    share = share.transpose(2, 0, 1, 3).reshape(27, part, wide)
    grad_in = grad_in.reshape(slots, batch, strip, flat).transpose(1, 0, 2, 3)
    return grad_in, share


def solution(mesh):
    return jax.shard_map(
        body,
        mesh=mesh,
        in_specs=(
            P("groups", "tm", "rows", None),
            P("groups", "tm", "rows", None),
            P(),
            P("groups"),
        ),
        out_specs=(P("groups", "tm", "rows", None), P("groups", "tm", "rows")),
        check_vma=False,
    )
```

```python
import functools

import jax
import jax.numpy as jnp
from jax import lax
from jax.experimental import pallas as pl
from jax.experimental.pallas import tpu as pltpu
from jax.sharding import PartitionSpec as P

CH = 192
PAIR = 2 * CH
MESH = pl.DeviceIdType.MESH

CUTS = ((0, 5), (5, 9))


def kernel_body(cells, strips, spans, factor, x_ref, mask_ref, own_ref, kern_ref,
                out_ref, share0_ref, share1_ref, xc, act, act3, gc, wg, got1, send2, got2,
                zfull0, zfull1, zsend0, zsend1, got30, got31, near, s1, r1, s2, r2, s3, r3, sn, rn):
    frames = x_ref.shape[0]
    tail = own_ref.shape[0] - frames
    batch = tail // 2
    pairs = cells // 2
    wide, part, half = CH // strips, CH // spans, strips // 2
    share, zfull, zsend, got3 = (share0_ref, share1_ref), (zfull0, zfull1), (zsend0, zsend1), (got30, got31)
    row = lax.axis_index("rows")
    span = lax.axis_index("tm")
    place = row // 2
    parity = row - 2 * place
    other = 1 - parity
    partner = 2 * place + other

    def strip_at(d):
        return lax.rem(place + d, half)

    barrier = pltpu.get_barrier_semaphore()
    for d in range(1, strips):
        pl.semaphore_signal(barrier, inc=1, device_id={"rows": lax.rem(row + d, strips)}, device_id_type=MESH)
    for d in range(1, spans):
        pl.semaphore_signal(barrier, inc=1, device_id={"tm": lax.rem(span + d, spans)}, device_id_type=MESH)

    pl.semaphore_wait(barrier, strips + spans - 2)
    has_above, has_below = row > 0, row < strips - 1
    near_copies = [
        pltpu.make_async_remote_copy(
            own_ref, near.at[n], sn.at[n], rn.at[n],
            device_id={"rows": lax.rem(row + strips + move, strips)}, device_id_type=MESH,
        )
        for n, move in enumerate((-1, 1))
    ]
    pl.when(has_above)(near_copies[0].start)
    pl.when(has_below)(near_copies[1].start)

    live = mask_ref[...] > 0.5

    def split(p, carry):
        at = pl.multiple_of(p * PAIR, 128)
        v = x_ref[:, pl.ds(at, PAIR)]
        for q in range(2):
            cell = v[:, q * CH:(q + 1) * CH]
            xc[2 * p + q] = cell
            xf = cell.astype(jnp.float32)
            s = 1.0 / (1.0 + jnp.exp(-xf))
            act[2 * p + q + 1] = jnp.where(live, xf * s, 0.0).astype(jnp.bfloat16)
        return split_row(own_ref, 0, p, carry)

    def split_row(ref, b, p, carry):
        at = pl.multiple_of(p * PAIR, 128)
        v = ref[:, pl.ds(at, PAIR)]
        for q in range(2):
            cell = v[:, q * CH:(q + 1) * CH]
            for a in range(3):
                lo = (2 - a) * batch
                gc[3 * b + a, 2 * p + q + 1] = cell[lo:lo + frames]
        return carry

    def split_near(p, carry):
        for n in range(2):
            split_row(near.at[n], n + 1, p, carry)
        return carry

    zero = jnp.zeros((frames, CH), jnp.bfloat16)
    for end in (0, cells + 1):
        act[end] = zero
        for k in range(9):
            gc[k, end] = zero
    lax.fori_loop(0, pairs, split, 0)

    def widen(w, carry):
        act3[w] = jnp.concatenate([act[w], act[w + 1], act[w + 2]], axis=1)
        return carry

    lax.fori_loop(0, cells, widen, 0)
    order = list(range(1, half)) + [0]
    copies1, copies2, copies3 = {}, {}, {}

    def weight(k, carry):
        g = gc[k, pl.ds(1, cells)].reshape(cells * frames, CH)
        a3 = act3[...].reshape(cells * frames, 3 * CH)
        res = lax.dot_general(g, a3, (((0,), (0,)), ((), ())), preferred_element_type=jnp.float32)
        for r in range(strips):
            wg[r, k] = res[r * wide:(r + 1) * wide]
        return carry

    def start_core(n):
        k0, k1 = CUTS[n]
        copies1[n] = []
        for d in order:
            cp = pltpu.make_async_remote_copy(
                wg.at[2 * strip_at(d) + other, pl.ds(k0, k1 - k0)], got1.at[d, pl.ds(k0, k1 - k0)],
                s1.at[n, d], r1.at[n, d], device_id={"rows": partner}, device_id_type=MESH,
            )
            cp.start()
            copies1[n].append(cp)

    def start_rows(n):
        k0, k1 = CUTS[n]
        copies2[n] = []
        for d, cp in zip(order, copies1[n]):
            cp.wait()
            if d:
                to = 2 * strip_at(d) + parity
                send2[d - 1, k0:k1] = (wg[to, k0:k1] + got1[d, k0:k1]).astype(jnp.bfloat16)
                nxt = pltpu.make_async_remote_copy(
                    send2.at[d - 1, pl.ds(k0, k1 - k0)], got2.at[d - 1, pl.ds(k0, k1 - k0)],
                    s2.at[n, d - 1], r2.at[n, d - 1], device_id={"rows": to}, device_id_type=MESH,
                )
                nxt.start()
                copies2[n].append(nxt)

    def start_spans(n):
        k0, k1 = CUTS[n]
        total = wg[row, k0:k1] + got1[0, k0:k1]
        for d, cp in enumerate(copies2[n]):
            cp.wait()
            total = total + got2[d, k0:k1].astype(jnp.float32)
        turned = total.reshape((k1 - k0) * wide, 3 * CH).T
        for t in range(spans):
            for c in range(3):
                piece = turned[c * CH + t * part:c * CH + (t + 1) * part]
                zfull[n][t, c] = piece
                zsend[n][t, c] = piece.astype(jnp.bfloat16)
        copies3[n] = []
        for d in range(1, spans):
            to = lax.rem(span + d, spans)
            cp = pltpu.make_async_remote_copy(
                zsend[n].at[to], got3[n].at[d - 1], s3.at[n, d - 1], r3.at[n, d - 1],
                device_id={"tm": to}, device_id_type=MESH,
            )
            cp.start()
            copies3[n].append(cp)

    def finish(n):
        final = zfull[n][span]
        for d, cp in enumerate(copies3[n]):
            cp.wait()
            final = final + got3[n][d].astype(jnp.float32)
        share[n][...] = final * factor

    step = 26 if cells % 26 == 0 else 2
    steps = cells // step

    def adjoint(j, carry):
        w0 = j * step
        acc = jnp.zeros((step * frames, CH), jnp.float32)
        for k in range(9):
            for c in range(3):
                g = gc[k, pl.ds(w0 + 2 - c, step)].reshape(step * frames, CH)
                acc = acc + lax.dot_general(
                    g, kern_ref[9 * (k % 3) + 3 * (1, 0, 2)[k // 3] + c], (((1,), (1,)), ((), ())), preferred_element_type=jnp.float32
                )
        acc = acc.reshape(step, frames, CH)
        xf = xc[pl.ds(w0, step)].astype(jnp.float32)
        s = 1.0 / (1.0 + jnp.exp(-xf))
        res = jnp.where(live[None], acc * (s * (1.0 + xf * (1.0 - s))), 0.0).astype(jnp.bfloat16)
        for p in range(step // 2):
            at = pl.multiple_of((w0 + 2 * p) * CH, 128)
            out_ref[:, pl.ds(at, PAIR)] = jnp.concatenate([res[2 * p], res[2 * p + 1]], axis=1)
        return carry

    lax.fori_loop(0, 3, weight, 0)

    @pl.when(has_below)
    def _():
        near_copies[0].wait_recv()

    @pl.when(has_above)
    def _():
        near_copies[0].wait_send()
        near_copies[1].wait_recv()

    @pl.when(has_below)
    def _():
        near_copies[1].wait_send()

    @pl.when(row == strips - 1)
    def _():
        near[0] = jnp.zeros(near.shape[1:], near.dtype)

    @pl.when(row == 0)
    def _():
        near[1] = jnp.zeros(near.shape[1:], near.dtype)

    lax.fori_loop(0, pairs, split_near, 0)
    lax.fori_loop(3, CUTS[0][1], weight, 0)
    start_core(0)
    lax.fori_loop(*CUTS[1], weight, 0)
    start_core(1)
    start_rows(0)
    lax.fori_loop(0, steps // 4, adjoint, 0)
    start_rows(1)
    lax.fori_loop(steps // 4, 3 * steps // 4, adjoint, 0)
    start_spans(0)
    lax.fori_loop(3 * steps // 4, steps, adjoint, 0)
    start_spans(1)
    finish(0)
    finish(1)


def body(inputs, cotangent, kernel, span_frames):
    batch, slots, strip, flat = inputs.shape
    cells = flat // CH
    frames = batch * slots
    assert strip == 1 and cells % 2 == 0 and frames % 16 == 0
    spans, strips = lax.axis_size("tm"), lax.axis_size("rows")
    assert strips % 2 == 0 and CH % spans == 0 and CH % strips == 0
    span = lax.axis_index("tm")
    count = jnp.sum(jnp.where(jnp.arange(span_frames.shape[0], dtype=jnp.int32) == span, span_frames, 0))
    x = inputs.reshape(batch, slots, flat).transpose(1, 0, 2).reshape(frames, flat)
    cot = cotangent.reshape(batch, slots, flat).transpose(1, 0, 2)

    back = [(i + 1, i) for i in range(spans - 1)]
    after_one = lax.ppermute(cot[0], "tm", back)
    after_two = lax.ppermute(jnp.where(count >= 2, cot[1], after_one), "tm", back)
    order = jnp.arange(slots + 2, dtype=jnp.int32)[:, None, None]
    ext = jnp.pad(cot, ((0, 2), (0, 0), (0, 0)))
    ext = jnp.where(order < count, ext, jnp.zeros_like(ext))
    ext = jnp.where(order == count, after_one[None], ext)
    ext = jnp.where(order == count + 1, after_two[None], ext)
    ext = ext.reshape(frames + 2 * batch, flat)
    live = jnp.arange(frames, dtype=jnp.int32) < count * batch
    mask = jnp.broadcast_to(live[:, None], (frames, CH)).astype(jnp.float32)

    vmem = pl.BlockSpec(memory_space=pltpu.VMEM)
    wide, part, half = CH // strips, CH // spans, strips // 2
    total_cells = batch * slots * spans * strip * strips * cells
    few, some = max(half - 1, 1), max(spans - 1, 1)
    sizes = [k1 - k0 for k0, k1 in CUTS]
    zblocks = [(3, part, n * wide) for n in sizes]
    dma = pltpu.SemaphoreType.DMA
    block = (9, wide, 3 * CH)
    grad_in, *shares = pl.pallas_call(
        functools.partial(kernel_body, cells, strips, spans, float(total_cells) ** -0.5),
        out_shape=(
            jax.ShapeDtypeStruct((frames, flat), jnp.bfloat16),
            jax.ShapeDtypeStruct(zblocks[0], jnp.float32),
            jax.ShapeDtypeStruct(zblocks[1], jnp.float32),
        ),
        in_specs=[vmem] * 4,
        out_specs=(vmem, vmem, vmem),
        scratch_shapes=[
            pltpu.VMEM((cells, frames, CH), jnp.bfloat16),
            pltpu.VMEM((cells + 2, frames, CH), jnp.bfloat16),
            pltpu.VMEM((cells, frames, 3 * CH), jnp.bfloat16),
            pltpu.VMEM((9, cells + 2, frames, CH), jnp.bfloat16),
            pltpu.VMEM((strips,) + block, jnp.float32),
            pltpu.VMEM((half,) + block, jnp.float32),
            pltpu.VMEM((few,) + block, jnp.bfloat16),
            pltpu.VMEM((few,) + block, jnp.bfloat16),
            pltpu.VMEM((spans,) + zblocks[0], jnp.float32),
            pltpu.VMEM((spans,) + zblocks[1], jnp.float32),
            pltpu.VMEM((spans,) + zblocks[0], jnp.bfloat16),
            pltpu.VMEM((spans,) + zblocks[1], jnp.bfloat16),
            pltpu.VMEM((some,) + zblocks[0], jnp.bfloat16),
            pltpu.VMEM((some,) + zblocks[1], jnp.bfloat16),
            pltpu.VMEM((2, frames + 2 * batch, flat), jnp.bfloat16),
            dma((2, half)), dma((2, half)), dma((2, few)), dma((2, few)), dma((2, some)), dma((2, some)),
            dma((2,)), dma((2,)),
        ],
        compiler_params=pltpu.CompilerParams(
            vmem_limit_bytes=56 << 20, collective_id=0, has_side_effects=True
        ),
        name="fused",
    )(x, mask, ext, kernel)
    share = jnp.concatenate([s.reshape(3, part, n, wide) for s, n in zip(shares, sizes)], axis=2)
    share = share.reshape(3, part, 3, 3, wide)
    share = jnp.concatenate([share[:, :, 1:2], share[:, :, 0:1], share[:, :, 2:3]], axis=2)
    share = share.transpose(3, 2, 0, 1, 4).reshape(27, part, wide)
    grad_in = grad_in.reshape(slots, batch, strip, flat).transpose(1, 0, 2, 3)
    return grad_in, share


def solution(mesh):
    return jax.shard_map(
        body,
        mesh=mesh,
        in_specs=(
            P("groups", "tm", "rows", None),
            P("groups", "tm", "rows", None),
            P(),
            P("groups"),
        ),
        out_specs=(P("groups", "tm", "rows", None), P("groups", "tm", "rows")),
        check_vma=False,
    )
```

```python
import functools

import jax
import jax.numpy as jnp
from jax import lax
from jax.experimental import pallas as pl
from jax.experimental.pallas import tpu as pltpu
from jax.sharding import PartitionSpec as P

CH = 192
PAIR = 2 * CH
MESH = pl.DeviceIdType.MESH

CUTS = ((0, 3), (3, 6), (6, 9))


def kernel_body(cells, strips, spans, factor, x_ref, mask_ref, own_ref, kern_ref,
                out_ref, share_ref, xc, act, act3, gc, wg, got1, send2, got2,
                zfull, zsend, got3, near, s1, r1, s2, r2, s3, r3, sn, rn):
    frames = x_ref.shape[0]
    tail = own_ref.shape[0] - frames
    batch = tail // 2
    pairs = cells // 2
    wide, part, half = CH // strips, CH // spans, strips // 2
    row = lax.axis_index("rows")
    span = lax.axis_index("tm")
    place = row // 2
    parity = row - 2 * place
    other = 1 - parity
    partner = 2 * place + other

    def strip_at(d):
        return lax.rem(place + d, half)

    barrier = pltpu.get_barrier_semaphore()
    for d in range(1, strips):
        pl.semaphore_signal(barrier, inc=1, device_id={"rows": lax.rem(row + d, strips)}, device_id_type=MESH)
    for d in range(1, spans):
        pl.semaphore_signal(barrier, inc=1, device_id={"tm": lax.rem(span + d, spans)}, device_id_type=MESH)

    pl.semaphore_wait(barrier, strips + spans - 2)
    has_above, has_below = row > 0, row < strips - 1
    near_copies = [
        pltpu.make_async_remote_copy(
            own_ref, near.at[n], sn.at[n], rn.at[n],
            device_id={"rows": lax.rem(row + strips + move, strips)}, device_id_type=MESH,
        )
        for n, move in enumerate((-1, 1))
    ]
    pl.when(has_above)(near_copies[0].start)
    pl.when(has_below)(near_copies[1].start)

    live = mask_ref[...] > 0.5

    def split(p, carry):
        at = pl.multiple_of(p * PAIR, 128)
        v = x_ref[:, pl.ds(at, PAIR)]
        for q in range(2):
            cell = v[:, q * CH:(q + 1) * CH]
            xc[2 * p + q] = cell
            xf = cell.astype(jnp.float32)
            s = 1.0 / (1.0 + jnp.exp(-xf))
            act[2 * p + q + 1] = jnp.where(live, xf * s, 0.0).astype(jnp.bfloat16)
        return split_row(own_ref, 0, p, carry)

    def split_row(ref, b, p, carry):
        at = pl.multiple_of(p * PAIR, 128)
        v = ref[:, pl.ds(at, PAIR)]
        for q in range(2):
            cell = v[:, q * CH:(q + 1) * CH]
            for a in range(3):
                lo = (2 - a) * batch
                gc[3 * b + a, 2 * p + q + 1] = cell[lo:lo + frames]
        return carry

    def split_near(p, carry):
        for n in range(2):
            split_row(near.at[n], n + 1, p, carry)
        return carry

    zero = jnp.zeros((frames, CH), jnp.bfloat16)
    for end in (0, cells + 1):
        act[end] = zero
        for k in range(9):
            gc[k, end] = zero
    lax.fori_loop(0, pairs, split, 0)

    def widen(w, carry):
        act3[w] = jnp.concatenate([act[w], act[w + 1], act[w + 2]], axis=1)
        return carry

    lax.fori_loop(0, cells, widen, 0)
    order = list(range(1, half)) + [0]
    copies1, copies2, copies3 = {}, {}, {}

    def weight(k, carry):
        g = gc[k, pl.ds(1, cells)].reshape(cells * frames, CH)
        a3 = act3[...].reshape(cells * frames, 3 * CH)
        res = lax.dot_general(g, a3, (((0,), (0,)), ((), ())), preferred_element_type=jnp.float32)
        for r in range(strips):
            wg[r, k] = res[r * wide:(r + 1) * wide]
        return carry

    def start_core(n):
        k0, k1 = CUTS[n]
        copies1[n] = []
        for d in order:
            cp = pltpu.make_async_remote_copy(
                wg.at[2 * strip_at(d) + other, pl.ds(k0, k1 - k0)], got1.at[d, pl.ds(k0, k1 - k0)],
                s1.at[n, d], r1.at[n, d], device_id={"rows": partner}, device_id_type=MESH,
            )
            cp.start()
            copies1[n].append(cp)

    def start_rows(n):
        k0, k1 = CUTS[n]
        copies2[n] = []
        for d, cp in zip(order, copies1[n]):
            cp.wait()
            if d:
                to = 2 * strip_at(d) + parity
                send2[d - 1, k0:k1] = (wg[to, k0:k1] + got1[d, k0:k1]).astype(jnp.bfloat16)
                nxt = pltpu.make_async_remote_copy(
                    send2.at[d - 1, pl.ds(k0, k1 - k0)], got2.at[d - 1, pl.ds(k0, k1 - k0)],
                    s2.at[n, d - 1], r2.at[n, d - 1], device_id={"rows": to}, device_id_type=MESH,
                )
                nxt.start()
                copies2[n].append(nxt)

    def start_spans(n):
        k0, k1 = CUTS[n]
        total = wg[row, k0:k1] + got1[0, k0:k1]
        for d, cp in enumerate(copies2[n]):
            cp.wait()
            total = total + got2[d, k0:k1].astype(jnp.float32)
        turned = total.reshape((k1 - k0) * wide, 3 * CH).T
        for t in range(spans):
            piece = jnp.concatenate(
                [turned[c * CH + t * part:c * CH + (t + 1) * part] for c in range(3)], axis=1
            )
            zfull[n, t] = piece
            zsend[n, t] = piece.astype(jnp.bfloat16)
        copies3[n] = []
        for d in range(1, spans):
            to = lax.rem(span + d, spans)
            cp = pltpu.make_async_remote_copy(
                zsend.at[n, to], got3.at[n, d - 1], s3.at[n, d - 1], r3.at[n, d - 1],
                device_id={"tm": to}, device_id_type=MESH,
            )
            cp.start()
            copies3[n].append(cp)

    def finish(n):
        final = zfull[n, span]
        for d, cp in enumerate(copies3[n]):
            cp.wait()
            final = final + got3[n, d].astype(jnp.float32)
        share_ref[n] = final * factor

    step = 26 if cells % 26 == 0 else 2
    steps = cells // step

    def adjoint(j, carry):
        w0 = j * step
        acc = jnp.zeros((step * frames, CH), jnp.float32)
        for k in range(9):
            for c in range(3):
                g = gc[k, pl.ds(w0 + 2 - c, step)].reshape(step * frames, CH)
                acc = acc + lax.dot_general(
                    g, kern_ref[9 * (k % 3) + 3 * (1, 0, 2)[k // 3] + c], (((1,), (1,)), ((), ())), preferred_element_type=jnp.float32
                )
        acc = acc.reshape(step, frames, CH)
        xf = xc[pl.ds(w0, step)].astype(jnp.float32)
        s = 1.0 / (1.0 + jnp.exp(-xf))
        res = jnp.where(live[None], acc * (s * (1.0 + xf * (1.0 - s))), 0.0).astype(jnp.bfloat16)
        for p in range(step // 2):
            at = pl.multiple_of((w0 + 2 * p) * CH, 128)
            out_ref[:, pl.ds(at, PAIR)] = jnp.concatenate([res[2 * p], res[2 * p + 1]], axis=1)
        return carry

    lax.fori_loop(*CUTS[0], weight, 0)
    start_core(0)
    start_rows(0)

    @pl.when(has_below)
    def _():
        near_copies[0].wait_recv()

    @pl.when(has_above)
    def _():
        near_copies[0].wait_send()
        near_copies[1].wait_recv()

    @pl.when(has_below)
    def _():
        near_copies[1].wait_send()

    @pl.when(row == strips - 1)
    def _():
        near[0] = jnp.zeros(near.shape[1:], near.dtype)

    @pl.when(row == 0)
    def _():
        near[1] = jnp.zeros(near.shape[1:], near.dtype)

    lax.fori_loop(0, pairs, split_near, 0)
    lax.fori_loop(*CUTS[1], weight, 0)
    start_core(1)
    start_spans(0)
    lax.fori_loop(*CUTS[2], weight, 0)
    start_core(2)
    start_rows(1)
    lax.fori_loop(0, steps // 4, adjoint, 0)
    start_rows(2)
    lax.fori_loop(steps // 4, 3 * steps // 4, adjoint, 0)
    start_spans(1)
    lax.fori_loop(3 * steps // 4, steps, adjoint, 0)
    start_spans(2)
    for n in range(3):
        finish(n)


def body(inputs, cotangent, kernel, span_frames):
    batch, slots, strip, flat = inputs.shape
    cells = flat // CH
    frames = batch * slots
    assert strip == 1 and cells % 2 == 0 and frames % 16 == 0
    spans, strips = lax.axis_size("tm"), lax.axis_size("rows")
    assert strips % 2 == 0 and CH % spans == 0 and CH % strips == 0
    span = lax.axis_index("tm")
    count = jnp.sum(jnp.where(jnp.arange(span_frames.shape[0], dtype=jnp.int32) == span, span_frames, 0))
    x = inputs.reshape(batch, slots, flat).transpose(1, 0, 2).reshape(frames, flat)
    cot = cotangent.reshape(batch, slots, flat).transpose(1, 0, 2)

    back = [(i + 1, i) for i in range(spans - 1)]
    after_one = lax.ppermute(cot[0], "tm", back)
    after_two = lax.ppermute(jnp.where(count >= 2, cot[1], after_one), "tm", back)
    order = jnp.arange(slots + 2, dtype=jnp.int32)[:, None, None]
    ext = jnp.pad(cot, ((0, 2), (0, 0), (0, 0)))
    ext = jnp.where(order < count, ext, jnp.zeros_like(ext))
    ext = jnp.where(order == count, after_one[None], ext)
    ext = jnp.where(order == count + 1, after_two[None], ext)
    ext = ext.reshape(frames + 2 * batch, flat)
    live = jnp.arange(frames, dtype=jnp.int32) < count * batch
    mask = jnp.broadcast_to(live[:, None], (frames, CH)).astype(jnp.float32)

    vmem = pl.BlockSpec(memory_space=pltpu.VMEM)
    wide, part, half = CH // strips, CH // spans, strips // 2
    total_cells = batch * slots * spans * strip * strips * cells
    few, some = max(half - 1, 1), max(spans - 1, 1)
    zblock = (part, 9 * wide)
    dma = pltpu.SemaphoreType.DMA
    block = (9, wide, 3 * CH)
    grad_in, share = pl.pallas_call(
        functools.partial(kernel_body, cells, strips, spans, float(total_cells) ** -0.5),
        out_shape=(
            jax.ShapeDtypeStruct((frames, flat), jnp.bfloat16),
            jax.ShapeDtypeStruct((3,) + zblock, jnp.float32),
        ),
        in_specs=[vmem] * 4,
        out_specs=(vmem, vmem),
        scratch_shapes=[
            pltpu.VMEM((cells, frames, CH), jnp.bfloat16),
            pltpu.VMEM((cells + 2, frames, CH), jnp.bfloat16),
            pltpu.VMEM((cells, frames, 3 * CH), jnp.bfloat16),
            pltpu.VMEM((9, cells + 2, frames, CH), jnp.bfloat16),
            pltpu.VMEM((strips,) + block, jnp.float32),
            pltpu.VMEM((half,) + block, jnp.float32),
            pltpu.VMEM((few,) + block, jnp.bfloat16),
            pltpu.VMEM((few,) + block, jnp.bfloat16),
            pltpu.VMEM((3, spans) + zblock, jnp.float32),
            pltpu.VMEM((3, spans) + zblock, jnp.bfloat16),
            pltpu.VMEM((3, some) + zblock, jnp.bfloat16),
            pltpu.VMEM((2, frames + 2 * batch, flat), jnp.bfloat16),
            dma((3, half)), dma((3, half)), dma((3, few)), dma((3, few)), dma((3, some)), dma((3, some)),
            dma((2,)), dma((2,)),
        ],
        compiler_params=pltpu.CompilerParams(
            vmem_limit_bytes=56 << 20, collective_id=0, has_side_effects=True
        ),
        name="fused",
    )(x, mask, ext, kernel)
    share = share.reshape(3, part, 3, 3, wide)
    share = jnp.stack([share[1], share[0], share[2]])
    share = share.transpose(3, 0, 2, 1, 4).reshape(27, part, wide)
    grad_in = grad_in.reshape(slots, batch, strip, flat).transpose(1, 0, 2, 3)
    return grad_in, share


def solution(mesh):
    return jax.shard_map(
        body,
        mesh=mesh,
        in_specs=(
            P("groups", "tm", "rows", None),
            P("groups", "tm", "rows", None),
            P(),
            P("groups"),
        ),
        out_specs=(P("groups", "tm", "rows", None), P("groups", "tm", "rows")),
        check_vma=False,
    )
```

```python
import functools

import jax
import jax.numpy as jnp
from jax import lax
from jax.experimental import pallas as pl
from jax.experimental.pallas import tpu as pltpu
from jax.sharding import PartitionSpec as P

CH = 192
PAIR = 2 * CH
MESH = pl.DeviceIdType.MESH

CUTS = ((0, 3), (3, 6), (6, 9))


def kernel_body(cells, strips, spans, factor, x_ref, mask_ref, own_ref, kern_ref,
                out_ref, share_ref, xc, act, act3, gc, wg, got1, send2, got2,
                zfull, zsend, got3, near, kern, sk, s1, r1, s2, r2, s3, r3, sn, rn):
    frames = x_ref.shape[0]
    tail = own_ref.shape[0] - frames
    batch = tail // 2
    pairs = cells // 2
    wide, part, half = CH // strips, CH // spans, strips // 2
    row = lax.axis_index("rows")
    span = lax.axis_index("tm")
    place = row // 2
    parity = row - 2 * place
    other = 1 - parity
    partner = 2 * place + other

    def strip_at(d):
        return lax.rem(place + d, half)

    barrier = pltpu.get_barrier_semaphore()
    for d in range(1, strips):
        pl.semaphore_signal(barrier, inc=1, device_id={"rows": lax.rem(row + d, strips)}, device_id_type=MESH)
    for d in range(1, spans):
        pl.semaphore_signal(barrier, inc=1, device_id={"tm": lax.rem(span + d, spans)}, device_id_type=MESH)

    pl.semaphore_wait(barrier, strips + spans - 2)
    has_above, has_below = row > 0, row < strips - 1
    near_copies = [
        pltpu.make_async_remote_copy(
            own_ref, near.at[n], sn.at[n], rn.at[n],
            device_id={"rows": lax.rem(row + strips + move, strips)}, device_id_type=MESH,
        )
        for n, move in enumerate((-1, 1))
    ]
    pl.when(has_above)(near_copies[0].start)
    pl.when(has_below)(near_copies[1].start)

    kern_copy = pltpu.make_async_copy(kern_ref, kern, sk)
    kern_copy.start()
    live = mask_ref[...] > 0.5

    def split(p, carry):
        at = pl.multiple_of(p * PAIR, 128)
        v = x_ref[:, pl.ds(at, PAIR)]
        for q in range(2):
            cell = v[:, q * CH:(q + 1) * CH]
            xc[2 * p + q] = cell
            xf = cell.astype(jnp.float32)
            s = 1.0 / (1.0 + jnp.exp(-xf))
            act[2 * p + q + 1] = jnp.where(live, xf * s, 0.0).astype(jnp.bfloat16)
        return split_row(own_ref, 0, p, carry)

    def split_row(ref, b, p, carry):
        at = pl.multiple_of(p * PAIR, 128)
        v = ref[:, pl.ds(at, PAIR)]
        for q in range(2):
            cell = v[:, q * CH:(q + 1) * CH]
            for a in range(3):
                lo = (2 - a) * batch
                gc[3 * b + a, 2 * p + q + 1] = cell[lo:lo + frames]
        return carry

    def split_near(p, carry):
        for n in range(2):
            split_row(near.at[n], n + 1, p, carry)
        return carry

    zero = jnp.zeros((frames, CH), jnp.bfloat16)
    for end in (0, cells + 1):
        act[end] = zero
        for k in range(9):
            gc[k, end] = zero
    lax.fori_loop(0, pairs, split, 0, unroll=2)

    def widen(w, carry):
        act3[w] = jnp.concatenate([act[w], act[w + 1], act[w + 2]], axis=1)
        return carry

    lax.fori_loop(0, cells, widen, 0, unroll=4)
    order = list(range(1, half)) + [0]
    copies1, copies2, copies3 = {}, {}, {}

    def weight(k, carry):
        g = gc[k, pl.ds(1, cells)].reshape(cells * frames, CH)
        a3 = act3[...].reshape(cells * frames, 3 * CH)
        res = lax.dot_general(g, a3, (((0,), (0,)), ((), ())), preferred_element_type=jnp.float32)
        for r in range(strips):
            wg[r, k] = res[r * wide:(r + 1) * wide]
        return carry

    def start_core(n):
        k0, k1 = CUTS[n]
        copies1[n] = []
        for d in order:
            cp = pltpu.make_async_remote_copy(
                wg.at[2 * strip_at(d) + other, pl.ds(k0, k1 - k0)], got1.at[d, pl.ds(k0, k1 - k0)],
                s1.at[n, d], r1.at[n, d], device_id={"rows": partner}, device_id_type=MESH,
            )
            cp.start()
            copies1[n].append(cp)

    def start_rows(n):
        k0, k1 = CUTS[n]
        copies2[n] = []
        for d, cp in zip(order, copies1[n]):
            cp.wait()
            if d:
                to = 2 * strip_at(d) + parity
                send2[d - 1, k0:k1] = (wg[to, k0:k1] + got1[d, k0:k1]).astype(jnp.bfloat16)
                nxt = pltpu.make_async_remote_copy(
                    send2.at[d - 1, pl.ds(k0, k1 - k0)], got2.at[d - 1, pl.ds(k0, k1 - k0)],
                    s2.at[n, d - 1], r2.at[n, d - 1], device_id={"rows": to}, device_id_type=MESH,
                )
                nxt.start()
                copies2[n].append(nxt)

    def start_spans(n):
        k0, k1 = CUTS[n]
        total = wg[row, k0:k1] + got1[0, k0:k1]
        for d, cp in enumerate(copies2[n]):
            cp.wait()
            total = total + got2[d, k0:k1].astype(jnp.float32)
        turned = total.reshape((k1 - k0) * wide, 3 * CH).T
        for t in range(spans):
            piece = jnp.concatenate(
                [turned[c * CH + t * part:c * CH + (t + 1) * part] for c in range(3)], axis=1
            )
            zfull[n, t] = piece
            zsend[n, t] = piece.astype(jnp.bfloat16)
        copies3[n] = []
        for d in range(1, spans):
            to = lax.rem(span + d, spans)
            cp = pltpu.make_async_remote_copy(
                zsend.at[n, to], got3.at[n, d - 1], s3.at[n, d - 1], r3.at[n, d - 1],
                device_id={"tm": to}, device_id_type=MESH,
            )
            cp.start()
            copies3[n].append(cp)

    def finish(n):
        final = zfull[n, span]
        for d, cp in enumerate(copies3[n]):
            cp.wait()
            final = final + got3[n, d].astype(jnp.float32)
        share_ref[n] = final * factor

    step = 26 if cells % 26 == 0 else 2
    steps = cells // step

    def adjoint(j, carry):
        w0 = j * step
        acc = jnp.zeros((step * frames, CH), jnp.float32)
        for k in range(9):
            for c in range(3):
                g = gc[k, pl.ds(w0 + 2 - c, step)].reshape(step * frames, CH)
                acc = acc + lax.dot_general(
                    g, kern[9 * (k % 3) + 3 * (1, 0, 2)[k // 3] + c], (((1,), (1,)), ((), ())), preferred_element_type=jnp.float32
                )
        acc = acc.reshape(step, frames, CH)
        xf = xc[pl.ds(w0, step)].astype(jnp.float32)
        s = 1.0 / (1.0 + jnp.exp(-xf))
        res = jnp.where(live[None], acc * (s * (1.0 + xf * (1.0 - s))), 0.0).astype(jnp.bfloat16)
        for p in range(step // 2):
            at = pl.multiple_of((w0 + 2 * p) * CH, 128)
            out_ref[:, pl.ds(at, PAIR)] = jnp.concatenate([res[2 * p], res[2 * p + 1]], axis=1)
        return carry

    lax.fori_loop(*CUTS[0], weight, 0)
    start_core(0)

    @pl.when(has_below)
    def _():
        near_copies[0].wait_recv()

    @pl.when(has_above)
    def _():
        near_copies[0].wait_send()
        near_copies[1].wait_recv()

    @pl.when(has_below)
    def _():
        near_copies[1].wait_send()

    @pl.when(row == strips - 1)
    def _():
        near[0] = jnp.zeros(near.shape[1:], near.dtype)

    @pl.when(row == 0)
    def _():
        near[1] = jnp.zeros(near.shape[1:], near.dtype)

    lax.fori_loop(0, pairs, split_near, 0, unroll=2)
    start_rows(0)
    lax.fori_loop(*CUTS[1], weight, 0)
    start_core(1)
    lax.fori_loop(*CUTS[2], weight, 0)
    start_core(2)
    start_rows(1)
    start_spans(0)
    kern_copy.wait()
    lax.fori_loop(0, steps // 4, adjoint, 0)
    start_rows(2)
    lax.fori_loop(steps // 4, steps // 2, adjoint, 0)
    start_spans(1)
    lax.fori_loop(steps // 2, 3 * steps // 4, adjoint, 0)
    start_spans(2)
    lax.fori_loop(3 * steps // 4, steps, adjoint, 0)
    for n in range(3):
        finish(n)


def body(inputs, cotangent, kernel, span_frames):
    batch, slots, strip, flat = inputs.shape
    cells = flat // CH
    frames = batch * slots
    assert strip == 1 and cells % 2 == 0 and frames % 16 == 0
    spans, strips = lax.axis_size("tm"), lax.axis_size("rows")
    assert strips % 2 == 0 and CH % spans == 0 and CH % strips == 0
    span = lax.axis_index("tm")
    count = jnp.sum(jnp.where(jnp.arange(span_frames.shape[0], dtype=jnp.int32) == span, span_frames, 0))
    x = inputs.reshape(batch, slots, flat).transpose(1, 0, 2).reshape(frames, flat)
    cot = cotangent.reshape(batch, slots, flat).transpose(1, 0, 2)

    back = [(i + 1, i) for i in range(spans - 1)]
    after_one = lax.ppermute(cot[0], "tm", back)
    after_two = lax.ppermute(jnp.where(count >= 2, cot[1], after_one), "tm", back)
    order = jnp.arange(slots + 2, dtype=jnp.int32)[:, None, None]
    ext = jnp.pad(cot, ((0, 2), (0, 0), (0, 0)))
    ext = jnp.where(order < count, ext, jnp.zeros_like(ext))
    ext = jnp.where(order == count, after_one[None], ext)
    ext = jnp.where(order == count + 1, after_two[None], ext)
    ext = ext.reshape(frames + 2 * batch, flat)
    live = jnp.arange(frames, dtype=jnp.int32) < count * batch
    mask = jnp.broadcast_to(live[:, None], (frames, CH)).astype(jnp.float32)

    vmem = pl.BlockSpec(memory_space=pltpu.VMEM)
    wide, part, half = CH // strips, CH // spans, strips // 2
    total_cells = batch * slots * spans * strip * strips * cells
    few, some = max(half - 1, 1), max(spans - 1, 1)
    zblock = (part, 9 * wide)
    dma = pltpu.SemaphoreType.DMA
    block = (9, wide, 3 * CH)
    grad_in, share = pl.pallas_call(
        functools.partial(kernel_body, cells, strips, spans, float(total_cells) ** -0.5),
        out_shape=(
            jax.ShapeDtypeStruct((frames, flat), jnp.bfloat16),
            jax.ShapeDtypeStruct((3,) + zblock, jnp.float32),
        ),
        in_specs=[vmem] * 3 + [pl.BlockSpec(memory_space=pl.ANY)],
        out_specs=(vmem, vmem),
        scratch_shapes=[
            pltpu.VMEM((cells, frames, CH), jnp.bfloat16),
            pltpu.VMEM((cells + 2, frames, CH), jnp.bfloat16),
            pltpu.VMEM((cells, frames, 3 * CH), jnp.bfloat16),
            pltpu.VMEM((9, cells + 2, frames, CH), jnp.bfloat16),
            pltpu.VMEM((strips,) + block, jnp.float32),
            pltpu.VMEM((half,) + block, jnp.float32),
            pltpu.VMEM((few,) + block, jnp.bfloat16),
            pltpu.VMEM((few,) + block, jnp.bfloat16),
            pltpu.VMEM((3, spans) + zblock, jnp.float32),
            pltpu.VMEM((3, spans) + zblock, jnp.bfloat16),
            pltpu.VMEM((3, some) + zblock, jnp.bfloat16),
            pltpu.VMEM((2, frames + 2 * batch, flat), jnp.bfloat16),
            pltpu.VMEM(kernel.shape, kernel.dtype), dma(()),
            dma((3, half)), dma((3, half)), dma((3, few)), dma((3, few)), dma((3, some)), dma((3, some)),
            dma((2,)), dma((2,)),
        ],
        compiler_params=pltpu.CompilerParams(
            vmem_limit_bytes=56 << 20, collective_id=0, has_side_effects=True
        ),
        name="fused",
    )(x, mask, ext, kernel)
    share = share.reshape(3, part, 3, 3, wide)
    share = jnp.stack([share[1], share[0], share[2]])
    share = share.transpose(3, 0, 2, 1, 4).reshape(27, part, wide)
    grad_in = grad_in.reshape(slots, batch, strip, flat).transpose(1, 0, 2, 3)
    return grad_in, share


def solution(mesh):
    return jax.shard_map(
        body,
        mesh=mesh,
        in_specs=(
            P("groups", "tm", "rows", None),
            P("groups", "tm", "rows", None),
            P(),
            P("groups"),
        ),
        out_specs=(P("groups", "tm", "rows", None), P("groups", "tm", "rows")),
        check_vma=False,
    )
```
